128 devices in a mesh: dp: 8 (over z, x_hi), ctx: 16 (over x_lo, y, core).
Axes of the slice: x: 4 (x_hi: 2, x_lo: 2; x = x_hi * 2 + x_lo), y: 4, z: 4, core: 2. Of those that a mesh axis runs over, the one named last changes fastest.
Arguments:
- events: bfloat16 [65536, 1024], P(('dp', 'ctx')), parts along dimension 0, may hold values from -48 to 48
- destination: int32 [65536], P(('dp', 'ctx')), parts along dimension 0, may hold values from 0 to 8191, as said below
- segment: int32 [65536], P(('dp', 'ctx')), parts along dimension 0, may hold values from 0 to 3, never falling along the last dimension, each value on 1 to 6144 neighbouring positions
- w_query: bfloat16 [1024, 1024], replicated, may hold values from -0.375 to 0.375
- key_weight: bfloat16 [1024, 256], replicated, may hold values from -0.1875 to 0.1875
- value_weight: bfloat16 [1024, 256], replicated, may hold values from -0.75 to 0.75
Outputs:
- attended: bfloat16 [65536, 1024], P(('dp', 'ctx')), parts along dimension 0
The draws below stay inside these ranges and needn't reach their ends.
There are 8 independent parts, one for each index of `dp`. The reference program is written for one: setup_inputs(seed, part) draws one part's arguments, and reference() takes and returns one part's arrays. A program takes and returns all parts, laid end to end along the dimension named above; an argument that names none is the same for every part. Nothing has to cross between parts.
Inputs may be any that keep to these rules, and one draw needn't show every extreme that they name: destination is a permutation that moves stored events in aligned blocks of 64 rows, keeping their order inside a block; the 8 blocks of one device land on 8 different devices' ranges of 512 packed positions, so at most 64 rows of one device reach one device's range.
All inputs are finite; a program needn't handle non-finite values.
Results may differ from the reference program's by a relative error of at most 0.0045.
The reference program's roundings to bfloat16 on the way count: a program that leaves them out, or rounds other values in their place, can miss the bound.
Values may be sent and summed in bfloat16 or wider, within the bound.
No kernel may reach another device: no remote copies, remote signals or barrier semaphores. Data moves between devices by JAX's collectives and lax.ppermute only.
A program may use at most 64 MiB of HBM per device.

```python
import math
import jax
import jax.numpy as jnp
import numpy as np
from jax import lax

MODEL_WIDTH = 1024
QUERY_HEADS = 8
KEY_VALUE_HEADS = 2
HEAD_SIZE = 128
TOK_DEV = 512
BLOCKS = 8
BLK = 64
SEQ = 8192


def draw_events(key, part):
    first = jax.random.fold_in(key, 0)
    value_rows = jnp.clip(jax.random.normal(first, (SEQ, MODEL_WIDTH), jnp.float32), -6.0, 6.0)
    return value_rows.astype(jnp.bfloat16)


def draw_destination(key, part):
    ndevices = SEQ // TOK_DEV
    first, second = jax.random.split(key)
    offsets = jax.random.permutation(first, ndevices)[:BLOCKS]
    slots = jax.vmap(lambda dev: jax.random.permutation(jax.random.fold_in(second, dev), BLOCKS))(jnp.arange(ndevices))
    token_rows = jnp.arange(SEQ, dtype=jnp.int32)
    source = token_rows // TOK_DEV
    block = token_rows % TOK_DEV // BLK
    inner = token_rows % BLK
    target = (source + offsets[block]) % ndevices
    place = slots[target, block]
    return (target * TOK_DEV + place * BLK + inner).astype(jnp.int32)


def length_profile(number_of, total, bound, lean):
    loads = [(1 << 20) // math.isqrt(rank ** lean) + 1 for rank in range(2, number_of + 1)]
    spare, given = total - bound - (number_of - 1), [1] * (number_of - 1)
    while spare > 0:
        free = [i for i in range(number_of - 1) if given[i] < bound]
        whole, left = sum([loads[i] for i in free]), spare
        for i in free:
            extra = min(bound - given[i], max(1, left * loads[i] // whole), spare)
            given[i] = given[i] + extra
            spare = spare - extra
    return np.array([bound] + given)


def ragged(own_key, count, total, bound, skew):
    if count == 2:
        one = jax.random.randint(own_key, (), max(1, total - bound), min(bound, total - 1) + 1)
        return jnp.stack([one, total - one])
    lengths = jnp.asarray(length_profile(count, total, bound, skew), jnp.int32)
    couples = (count - 1) // 2
    donor, sink = lengths[1:1 + 2 * couples:2], lengths[2:2 + 2 * couples:2]
    margin = jnp.minimum(donor - 1, bound - sink)
    moved = jax.random.randint(jax.random.fold_in(own_key, 1), (couples,), 0, 1 << 20) % (margin + 1)
    lengths = lengths.at[1:1 + 2 * couples:2].set(donor - moved).at[2:2 + 2 * couples:2].set(sink + moved)
    return lengths[jax.random.permutation(jax.random.fold_in(own_key, 2), count)]


def bell_draw(key, extent, deviation, reach, held_as=jnp.bfloat16):
    result = jax.random.normal(key, extent, jnp.float32) * deviation
    return jnp.minimum(jnp.maximum(result, -reach), reach).astype(held_as)


def setup_inputs(seed: int = 0, part: int = 0) -> dict:
    key_list = jax.random.split(jax.random.key(seed), 7)
    part_keys = jax.random.split(jax.random.fold_in(key_list[6], part), 7)
    events = draw_events(jax.random.fold_in(jax.random.fold_in(key_list[6], part), 71), part)
    destination = draw_destination(jax.random.fold_in(jax.random.fold_in(key_list[6], part), 71), part)
    segment = jnp.searchsorted(jnp.cumsum(ragged(part_keys[2], 4, SEQ, 3 * SEQ // 4, 0)), jnp.arange(SEQ), side="right").astype(jnp.int32)
    w_query = bell_draw(key_list[3], (MODEL_WIDTH, QUERY_HEADS * HEAD_SIZE), (MODEL_WIDTH // 4) ** -0.5, 0.375)
    key_weight = bell_draw(key_list[4], (MODEL_WIDTH, KEY_VALUE_HEADS * HEAD_SIZE), MODEL_WIDTH ** -0.5, 0.1875)
    value_weight = bell_draw(key_list[5], (MODEL_WIDTH, KEY_VALUE_HEADS * HEAD_SIZE), (MODEL_WIDTH // 16) ** -0.5, 0.75)
    return {"events": events, "destination": destination, "segment": segment, "w_query": w_query, "key_weight": key_weight, "value_weight": value_weight}


def reference(events, destination, segment, w_query, key_weight, value_weight):
    history_length = events.shape[0]
    packed = jnp.zeros_like(events).at[destination].set(events)
    query_rows = jnp.dot(packed, w_query, preferred_element_type=jnp.float32).astype(jnp.bfloat16)
    key_rows = jnp.dot(packed, key_weight, preferred_element_type=jnp.float32).astype(jnp.bfloat16)
    value_rows = jnp.dot(packed, value_weight, preferred_element_type=jnp.float32).astype(jnp.bfloat16)
    group_size = QUERY_HEADS // KEY_VALUE_HEADS
    score_scale = 1.0 / math.sqrt(HEAD_SIZE)
    gathered_keys = key_rows.astype(jnp.float32).reshape(history_length, KEY_VALUE_HEADS, HEAD_SIZE)
    gathered_values = value_rows.astype(jnp.float32).reshape(history_length, KEY_VALUE_HEADS, HEAD_SIZE)
    positions = jnp.arange(history_length, dtype=jnp.int32)
    token_span = min(512, history_length)

    def one_block(block):
        start = (block * token_span).astype(jnp.int32)
        token_rows = lax.dynamic_slice_in_dim(query_rows, start, token_span, 0).astype(jnp.float32)
        token_rows = token_rows.reshape(token_span, KEY_VALUE_HEADS, group_size, HEAD_SIZE)
        row_pos = start + jnp.arange(token_span, dtype=jnp.int32)
        row_seg = lax.dynamic_slice_in_dim(segment, start, token_span, 0)
        logit_scores = jnp.einsum('qxli,oxi->xlqo', token_rows, gathered_keys) * score_scale
        allowed = (segment[None, :] == row_seg[:, None]) & (positions[None, :] <= row_pos[:, None])
        logit_scores = jnp.where(allowed, logit_scores, -jnp.inf)
        rowmax = lax.optimization_barrier(jnp.max(logit_scores, axis=-1))
        expd = jnp.where(allowed, jnp.exp(logit_scores - rowmax[..., None]), 0.0)
        total_tokens = lax.optimization_barrier(jnp.sum(expd, axis=-1))
        softmax_weights = lax.optimization_barrier(expd.astype(jnp.bfloat16)).astype(jnp.float32)
        mixed_output = jnp.einsum('qlwc,cqh->qlwh', softmax_weights, gathered_values) / total_tokens[..., None]
        return mixed_output.transpose(2, 0, 1, 3).reshape(token_span, QUERY_HEADS * HEAD_SIZE).astype(jnp.bfloat16)
    blocks = lax.map(one_block, jnp.arange(history_length // token_span, dtype=jnp.int32))
    return blocks.reshape(history_length, QUERY_HEADS * HEAD_SIZE)
```

```python
import math

import jax
import jax.numpy as jnp
from jax import lax
from jax.experimental import pallas as pl
from jax.experimental.pallas import tpu as pltpu
from jax.sharding import PartitionSpec as P


QUERY_HEADS = 8
KEY_VALUE_HEADS = 2
HEAD_SIZE = 128
GROUP = QUERY_HEADS // KEY_VALUE_HEADS
BLK = 64
META = 16
NEGATIVE_FILL = -1e30
SCALE2 = math.log2(math.e) / math.sqrt(HEAD_SIZE)
TK = 1024
TQ = 512


VMEM = pltpu.VMEM
SMEM = pltpu.SMEM


def lower_bound(ref, value, size):
    low = jnp.int32(0)
    step = size
    while step >= 1:
        probe = low + step
        inside = probe <= size
        entry = ref[jnp.minimum(probe, size) - 1]
        low = jnp.where(inside & (entry < value), probe, low)
        step //= 2
    return low


def kv_kernel(core_ref, dest_ref, seg_ref, ev_ref, kw_ref, vw_ref, own_ref, send_ref):
    rows = ev_ref.shape[0]
    core = core_ref[0]
    events = ev_ref[...]
    keys = jnp.dot(events, kw_ref[...], preferred_element_type=jnp.float32).astype(jnp.bfloat16)
    values = jnp.dot(events, vw_ref[...], preferred_element_type=jnp.float32).astype(jnp.bfloat16)

    def put(ref, head):
        cols = slice(head * HEAD_SIZE, (head + 1) * HEAD_SIZE)
        ref[:rows, :HEAD_SIZE] = keys[:, cols]
        ref[:rows, HEAD_SIZE:] = values[:, cols]

    @pl.when(core == 0)
    def _():
        put(own_ref, 0)
        put(send_ref, 1)

    @pl.when(core != 0)
    def _():
        put(own_ref, 1)
        put(send_ref, 0)

    lane = lax.broadcasted_iota(jnp.int32, (META, 2 * HEAD_SIZE), 1)
    meta = jnp.zeros((META, 2 * HEAD_SIZE), jnp.int32)
    for b in range(rows // BLK):
        meta = jnp.where(lane == b, dest_ref[b * BLK] // BLK, meta)
    for s in range(3):
        below = lower_bound(seg_ref, s + 1, rows)
        first = jnp.minimum(below, rows // 2)
        meta = jnp.where(lane == 16 + 2 * s, first, meta)
        meta = jnp.where(lane == 17 + 2 * s, below - first, meta)
    packed = meta.astype(jnp.float32).astype(jnp.bfloat16)
    own_ref[rows : rows + META, :] = packed
    send_ref[rows:, :] = packed


def q_kernel(dest_ref, ev_ref, wq_ref, after_ref, out_ref, q_ref, sem):
    del after_ref
    rows = ev_ref.shape[0]
    half = GROUP * HEAD_SIZE
    for g in range(KEY_VALUE_HEADS):
        q_ref[g] = jnp.dot(
            ev_ref[...], wq_ref[:, g * half : (g + 1) * half], preferred_element_type=jnp.float32
        ).astype(jnp.bfloat16)
    copies = []
    for b in range(rows // BLK):
        target = dest_ref[b * BLK] // rows
        chip = target // 2
        side = target % 2
        for g in range(KEY_VALUE_HEADS):
            copies.append(
                pltpu.make_async_copy(
                    q_ref.at[g, pl.ds(b * BLK, BLK), :],
                    out_ref.at[chip * 2 + g, side],
                    sem.at[b * KEY_VALUE_HEADS + g],
                )
            )
            copies[-1].start()
    for copy in copies:
        copy.wait()


def attention_kernel(where_ref, *refs):
    shards = refs[:8]
    q_in_ref, own_out, send_out = refs[8:11]
    kv, v_t, q_buf, q_t, meta_bf, meta_int, table, m_ref, l_ref, acc_ref, sem, meta_sem = refs[11:]
    chip_x, chip_y, core = where_ref[0], where_ref[1], where_ref[2]
    per_dev = (kv.shape[0] - TK) // 16
    shard_rows = per_dev + META
    blocks = per_dev // BLK
    offsets = [(0, 0), (0, 3), (0, 1), (1, 0), (1, 3), (0, 2), (1, 1), (1, 2)]

    def source(i, h):
        return shards[i], h * shard_rows

    fetches = []
    for i in range(8):
        for h in range(2):
            ref, base = source(i, h)
            copy = pltpu.make_async_copy(
                ref.at[pl.ds(base + per_dev, META), :], meta_bf.at[i * 2 + h], meta_sem.at[i * 2 + h]
            )
            copy.start()
            fetches.append(copy)
    for copy in fetches:
        copy.wait()
    meta = meta_bf[:, 0, :HEAD_SIZE].astype(jnp.float32).astype(jnp.int32)
    lane = lax.broadcasted_iota(jnp.int32, meta.shape, 1)
    total = jnp.sum(meta, axis=0, keepdims=True)
    meta_int[...] = jnp.where(lane < 16, meta, jnp.broadcast_to(total, meta.shape))
    copy = pltpu.make_async_copy(meta_int, table, meta_sem.at[0])
    copy.start()
    copy.wait()

    my_chip = chip_x * 4 + chip_y
    for i, (dx, dy) in enumerate(offsets):
        chip = (chip_x + dx) % 2 * 4 + (chip_y + dy) % 4
        for h in range(2):
            ref, base = source(i, h)
            device = chip * 2 + (core if h == 0 else 1 - core)

            def place(b, carry, ref=ref, base=base, device=device, i=i, h=h):
                j = table[i * 2 + h, b]
                pltpu.make_async_copy(
                    ref.at[pl.ds(base + b * BLK, BLK), :], kv.at[pl.ds(j * BLK, BLK), :], sem.at[0]
                ).start()

                @pl.when(j // (2 * blocks) == my_chip)
                def _():
                    local = j - my_chip * 2 * blocks
                    pltpu.make_async_copy(
                        q_in_ref.at[device, local // blocks], q_buf.at[pl.ds(local * BLK, BLK), :], sem.at[1]
                    ).start()

                return carry

            lax.fori_loop(0, blocks, place, 0)
    bound = [table[0, 16 + 2 * s] + table[0, 17 + 2 * s] for s in range(3)]

    def start_of(pos):
        begin = jnp.zeros_like(pos)
        for b in bound:
            begin = jnp.where(pos >= b, jnp.maximum(begin, b), begin)
        return begin

    rows_all = pl.ds(0, 16 * per_dev)
    kv[16 * per_dev :, :] = jnp.zeros((TK, 2 * HEAD_SIZE), jnp.bfloat16)
    pltpu.make_async_copy(kv.at[rows_all], kv.at[rows_all], sem.at[0]).wait()
    pltpu.make_async_copy(q_buf, q_buf, sem.at[1]).wait()

    chip_rows = 2 * per_dev
    first = my_chip * chip_rows
    anchor = start_of(first) // BLK * BLK

    def turn(t, carry):
        rows = pl.ds(pl.multiple_of(anchor + t * TK, BLK), TK)
        v_t[t] = kv[rows, HEAD_SIZE:].T
        return carry

    lax.fori_loop(0, (first + chip_rows - anchor + TK - 1) // TK, turn, 0)

    for tq in range(chip_rows // TQ):
        p0 = first + tq * TQ
        low_first = start_of(p0)
        low_last = start_of(p0 + TQ - 1)
        for h in range(GROUP):
            q = q_buf[tq * TQ : (tq + 1) * TQ, h * HEAD_SIZE : (h + 1) * HEAD_SIZE]
            q = q.astype(jnp.float32) * SCALE2
            high = q.astype(jnp.bfloat16)
            q_t[h, :HEAD_SIZE] = high.T
            q_t[h, HEAD_SIZE:] = (q - high.astype(jnp.float32)).astype(jnp.bfloat16).T
            m_ref[h] = jnp.full((1, TQ), NEGATIVE_FILL, jnp.float32)
            l_ref[h] = jnp.zeros((1, TQ), jnp.float32)
            acc_ref[h] = jnp.zeros((HEAD_SIZE, TQ), jnp.float32)

        def tile(t, masked, p0=p0):
            k0 = pl.multiple_of(anchor + t * TK, BLK)
            k = kv[pl.ds(k0, TK), :HEAD_SIZE]
            k = jnp.concatenate([k, k], axis=1)
            v = v_t[t]
            if masked:
                kpos = k0 + lax.broadcasted_iota(jnp.int32, (TK, TQ), 0)
                qpos = p0 + lax.broadcasted_iota(jnp.int32, (1, TQ), 1)
                allowed = (kpos <= qpos) & (kpos >= start_of(qpos))

            def score(h):
                s = jnp.dot(k, q_t[h], preferred_element_type=jnp.float32)
                return jnp.where(allowed, s, NEGATIVE_FILL) if masked else s

            s = score(0)
            for h in range(GROUP):
                following = score(h + 1) if h + 1 < GROUP else None
                m_old = m_ref[h]
                m_new = jnp.maximum(m_old, jnp.max(s, axis=0, keepdims=True))
                p = jnp.exp2(s - m_new)
                shrink = jnp.exp2(m_old - m_new)
                m_ref[h] = m_new
                l_ref[h] = l_ref[h] * shrink + jnp.sum(p, axis=0, keepdims=True)
                acc_ref[h] = acc_ref[h] * shrink + jnp.dot(
                    v, p.astype(jnp.bfloat16), preferred_element_type=jnp.float32
                )
                s = following

        def step(t, carry, tile=tile, p0=p0, low_last=low_last):
            k0 = anchor + t * TK
            clear = (k0 >= low_last) & (k0 + TK - 1 <= p0)

            @pl.when(clear)
            def _():
                tile(t, False)

            @pl.when(jnp.logical_not(clear))
            def _():
                tile(t, True)

            return carry

        lax.fori_loop((low_first - anchor) // TK, (p0 + TQ - 1 - anchor) // TK + 1, step, 0)
        side = tq * TQ // per_dev
        r0 = tq * TQ % per_dev
        parts = [(acc_ref[h] / l_ref[h]).T.astype(jnp.bfloat16) for h in range(GROUP)]

        def put(ref, c0, r0=r0, parts=parts):
            for h in range(GROUP):
                ref[r0 : r0 + TQ, c0 + h * HEAD_SIZE : c0 + (h + 1) * HEAD_SIZE] = parts[h]

        @pl.when(core == side)
        def _(put=put, side=side):
            put(own_out, side * GROUP * HEAD_SIZE)

        @pl.when(core != side)
        def _(put=put):
            put(send_out, 0)


def on_device(events, destination, segment, w_query, key_weight, value_weight):
    rows, width = events.shape
    ndev = lax.axis_size("ctx")
    me = lax.axis_index("ctx").astype(jnp.int32)
    core = me % 2
    chip_y = me // 2 % 4
    chip_x = me // 8
    half = GROUP * HEAD_SIZE
    shard = jax.ShapeDtypeStruct((rows + META, 2 * HEAD_SIZE), jnp.bfloat16)
    smem = pl.BlockSpec(memory_space=SMEM)
    vmem = pl.BlockSpec(memory_space=VMEM)
    hbm = pl.BlockSpec(memory_space=pl.ANY)

    def pairs(dx, dy, dc):
        return [
            (x * 8 + y * 2 + c, (x + dx) % 2 * 8 + (y + dy) % 4 * 2 + (c + dc) % 2)
            for x in range(2)
            for y in range(4)
            for c in range(2)
        ]

    up = lambda a: lax.ppermute(a, "ctx", pairs(0, 1, 0))
    down = lambda a: lax.ppermute(a, "ctx", pairs(0, -1, 0))
    across = lambda a: lax.ppermute(a, "ctx", pairs(1, 0, 0))
    swap = lambda a: lax.ppermute(a, "ctx", pairs(0, 0, 1))

    own, other = pl.pallas_call(
        kv_kernel,
        out_shape=(jax.ShapeDtypeStruct((2 * (rows + META), 2 * HEAD_SIZE), jnp.bfloat16), shard),
        in_specs=[smem, smem, smem, vmem, vmem, vmem],
        out_specs=(vmem, vmem),
        name="kv_projection",
    )(core[None], destination, segment, events, key_weight, value_weight)
    theirs = swap(other)
    q_send = pl.pallas_call(
        q_kernel,
        out_shape=jax.ShapeDtypeStruct((ndev, 2, BLK, half), jnp.bfloat16),
        in_specs=[smem, vmem, vmem, hbm],
        out_specs=hbm,
        scratch_shapes=[VMEM((2, rows, half), jnp.bfloat16), pltpu.SemaphoreType.DMA((rows // BLK * 2,))],
        name="query_projection",
    )(destination, events, w_query, own)
    mine = lax.dynamic_update_slice(own, theirs, (rows + META, 0))
    q_got = lax.all_to_all(q_send, "ctx", split_axis=0, concat_axis=0, tiled=True)
    y_down = up(mine)
    y_up = down(mine)
    x_far = across(mine)
    xd = up(x_far)
    y_two = down(y_up)
    xu = across(y_up)
    x_two = lax.ppermute(x_far, "ctx", pairs(0, 2, 0))
    out_half = jax.ShapeDtypeStruct((rows, half), jnp.bfloat16)
    mine_out, give_out = pl.pallas_call(
        attention_kernel,
        out_shape=(jax.ShapeDtypeStruct((rows, width), jnp.bfloat16), out_half),
        in_specs=[smem] + [hbm] * 9,
        out_specs=(vmem, vmem),
        scratch_shapes=[
            VMEM((ndev * rows + TK, 2 * HEAD_SIZE), jnp.bfloat16),
            VMEM((ndev * rows // TK + 1, HEAD_SIZE, TK), jnp.bfloat16),
            VMEM((2 * rows, half), jnp.bfloat16),
            VMEM((GROUP, 2 * HEAD_SIZE, TQ), jnp.bfloat16),
            VMEM((16, META, 2 * HEAD_SIZE), jnp.bfloat16),
            VMEM((16, HEAD_SIZE), jnp.int32),
            SMEM((16, HEAD_SIZE), jnp.int32),
            VMEM((GROUP, 1, TQ), jnp.float32),
            VMEM((GROUP, 1, TQ), jnp.float32),
            VMEM((GROUP, HEAD_SIZE, TQ), jnp.float32),
            pltpu.SemaphoreType.DMA((2,)),
            pltpu.SemaphoreType.DMA((16,)),
        ],
        name="attention",
    )(
        jnp.stack([chip_x, chip_y, core]),
        mine, y_down, y_up, x_far, xd, y_two, xu, x_two, q_got,
    )
    got = swap(give_out)
    return lax.dynamic_update_slice(mine_out, got, (jnp.int32(0), (1 - core) * half))


def solution(mesh):
    return jax.shard_map(
        on_device,
        mesh=mesh,
        in_specs=(P(("dp", "ctx"), None), P(("dp", "ctx")), P(("dp", "ctx")), P(), P(), P()),
        out_specs=P(("dp", "ctx"), None),
        check_vma=False,
    )
```

```python
import math

import jax
import jax.numpy as jnp
from jax import lax
from jax.experimental import pallas as pl
from jax.experimental.pallas import tpu as pltpu
from jax.sharding import PartitionSpec as P


QUERY_HEADS = 8
KEY_VALUE_HEADS = 2
HEAD_SIZE = 128
GROUP = QUERY_HEADS // KEY_VALUE_HEADS
BLK = 64
META = 16
NEGATIVE_FILL = -1e30
SCALE2 = math.log2(math.e) / math.sqrt(HEAD_SIZE)
TK = 1024
TQ = 512


VMEM = pltpu.VMEM
SMEM = pltpu.SMEM


def lower_bound(ref, value, size):
    low = jnp.int32(0)
    step = size
    while step >= 1:
        probe = low + step
        inside = probe <= size
        entry = ref[jnp.minimum(probe, size) - 1]
        low = jnp.where(inside & (entry < value), probe, low)
        step //= 2
    return low


def kv_kernel(core_ref, dest_ref, seg_ref, ev_ref, kw_ref, vw_ref, own_ref, send_ref):
    rows = ev_ref.shape[0]
    core = core_ref[0]
    events = ev_ref[...]
    keys = jnp.dot(events, kw_ref[...], preferred_element_type=jnp.float32).astype(jnp.bfloat16)
    values = jnp.dot(events, vw_ref[...], preferred_element_type=jnp.float32).astype(jnp.bfloat16)

    def put(ref, head):
        cols = slice(head * HEAD_SIZE, (head + 1) * HEAD_SIZE)
        ref[:rows, :HEAD_SIZE] = keys[:, cols]
        ref[:rows, HEAD_SIZE:] = values[:, cols]

    @pl.when(core == 0)
    def _():
        put(own_ref, 0)
        put(send_ref, 1)

    @pl.when(core != 0)
    def _():
        put(own_ref, 1)
        put(send_ref, 0)

    lane = lax.broadcasted_iota(jnp.int32, (META, 2 * HEAD_SIZE), 1)
    meta = jnp.zeros((META, 2 * HEAD_SIZE), jnp.int32)
    for b in range(rows // BLK):
        meta = jnp.where(lane == b, dest_ref[b * BLK] // BLK, meta)
    for s in range(3):
        below = lower_bound(seg_ref, s + 1, rows)
        first = jnp.minimum(below, rows // 2)
        meta = jnp.where(lane == 16 + 2 * s, first, meta)
        meta = jnp.where(lane == 17 + 2 * s, below - first, meta)
    packed = meta.astype(jnp.float32).astype(jnp.bfloat16)
    own_ref[rows : rows + META, :] = packed
    send_ref[rows:, :] = packed


def q_kernel(dest_ref, ev_ref, wq_ref, after_ref, out_ref, q_ref, sem):
    del after_ref
    rows = ev_ref.shape[0]
    half = GROUP * HEAD_SIZE
    for g in range(KEY_VALUE_HEADS):
        q_ref[g] = jnp.dot(
            ev_ref[...], wq_ref[:, g * half : (g + 1) * half], preferred_element_type=jnp.float32
        ).astype(jnp.bfloat16)
    copies = []
    for b in range(rows // BLK):
        target = dest_ref[b * BLK] // rows
        chip = target // 2
        side = target % 2
        for g in range(KEY_VALUE_HEADS):
            copies.append(
                pltpu.make_async_copy(
                    q_ref.at[g, pl.ds(b * BLK, BLK), :],
                    out_ref.at[chip * 2 + g, side],
                    sem.at[b * KEY_VALUE_HEADS + g],
                )
            )
            copies[-1].start()
    for copy in copies:
        copy.wait()


def attention_kernel(where_ref, *refs):
    shards = refs[:8]
    last_ref, q_in_ref, own_out, send_out = refs[8:12]
    kv, v_t, q_buf, q_t, meta_bf, meta_int, table, origin, m_ref, l_ref, acc_ref, sem, meta_sem = refs[12:]
    chip_x, chip_y, core = where_ref[0], where_ref[1], where_ref[2]
    per_dev = (kv.shape[0] - TK) // 16
    shard_rows = per_dev + META
    blocks = per_dev // BLK
    offsets = [(0, 0), (0, 3), (0, 1), (1, 0), (1, 3), (0, 2), (1, 1), (1, 2)]

    def source(i, h):
        if i < 7:
            return shards[i], h * shard_rows
        return (shards[7], 0) if h == 0 else (last_ref, 0)

    fetches = []
    for i in range(8):
        for h in range(2):
            ref, base = source(i, h)
            copy = pltpu.make_async_copy(
                ref.at[pl.ds(base + per_dev, META), :], meta_bf.at[i * 2 + h], meta_sem.at[i * 2 + h]
            )
            copy.start()
            fetches.append(copy)
    for copy in fetches:
        copy.wait()
    meta = meta_bf[:, 0, :HEAD_SIZE].astype(jnp.float32).astype(jnp.int32)
    lane = lax.broadcasted_iota(jnp.int32, meta.shape, 1)
    total = jnp.sum(meta, axis=0, keepdims=True)
    meta_int[...] = jnp.where(lane < 16, meta, jnp.broadcast_to(total, meta.shape))
    copy = pltpu.make_async_copy(meta_int, table, meta_sem.at[0])
    copy.start()
    copy.wait()

    my_chip = chip_x * 4 + chip_y
    for i, (dx, dy) in enumerate(offsets):
        chip = (chip_x + dx) % 2 * 4 + (chip_y + dy) % 4
        for h in range(2):
            ref, base = source(i, h)
            device = chip * 2 + (core if h == 0 else 1 - core)

            def place(b, carry, ref=ref, base=base, device=device, i=i, h=h):
                j = table[i * 2 + h, b]
                pltpu.make_async_copy(
                    ref.at[pl.ds(base + b * BLK, BLK), :], kv.at[pl.ds(j * BLK, BLK), :], sem.at[0]
                ).start()

                origin[j] = device
                return carry

            lax.fori_loop(0, blocks, place, 0, unroll=True)
    q_copies = []
    for n in range(2 * blocks):
        copy = pltpu.make_async_copy(
            q_in_ref.at[origin[my_chip * 2 * blocks + n], n // blocks],
            q_buf.at[n * BLK : (n + 1) * BLK, :],
            meta_sem.at[n],
        )
        copy.start()
        q_copies.append(copy)
    bound = [table[0, 16 + 2 * s] + table[0, 17 + 2 * s] for s in range(3)]

    def start_of(pos):
        begin = jnp.zeros_like(pos)
        for b in bound:
            begin = jnp.where(pos >= b, jnp.maximum(begin, b), begin)
        return begin

    rows_all = pl.ds(0, 16 * per_dev)
    kv[16 * per_dev :, :] = jnp.zeros((TK, 2 * HEAD_SIZE), jnp.bfloat16)

    chip_rows = 2 * per_dev
    first = my_chip * chip_rows
    anchor = start_of(first) // BLK * BLK

    for copy in q_copies:
        copy.wait()
    units = [(tq, h) for tq in range(chip_rows // TQ) for h in range(GROUP)]
    for u, (tq, h) in enumerate(units):
        q = q_buf[tq * TQ : (tq + 1) * TQ, h * HEAD_SIZE : (h + 1) * HEAD_SIZE]
        q = q.astype(jnp.float32) * SCALE2
        high = q.astype(jnp.bfloat16)
        q_t[u, :HEAD_SIZE] = high.T
        q_t[u, HEAD_SIZE:] = (q - high.astype(jnp.float32)).astype(jnp.bfloat16).T
        m_ref[u] = jnp.full((1, TQ), NEGATIVE_FILL, jnp.float32)
        l_ref[u] = jnp.zeros((1, TQ), jnp.float32)
        acc_ref[u] = jnp.zeros((HEAD_SIZE, TQ), jnp.float32)
    pltpu.make_async_copy(kv.at[rows_all], kv.at[rows_all], sem.at[0]).wait()

    def turn(t, carry):
        rows = pl.ds(pl.multiple_of(anchor + t * TK, BLK), TK)
        v_t[t] = kv[rows, HEAD_SIZE:].T
        return carry

    lax.fori_loop(0, (first + chip_rows - anchor + TK - 1) // TK, turn, 0)

    low_last = start_of(first + chip_rows - 1)

    def attend(work, k, v, allowed):
        def score(u):
            s = jnp.dot(k, q_t[u], preferred_element_type=jnp.float32)
            return s if allowed is None else jnp.where(allowed, s, NEGATIVE_FILL)

        s = score(work[0])
        for n, u in enumerate(work):
            following = score(work[n + 1]) if n + 1 < len(work) else None
            m_old = m_ref[u]
            m_new = jnp.maximum(m_old, jnp.max(s, axis=0, keepdims=True))
            p = jnp.exp2(s - m_new)
            shrink = jnp.exp2(m_old - m_new)
            m_ref[u] = m_new
            l_ref[u] = l_ref[u] * shrink + jnp.sum(p, axis=0, keepdims=True)
            acc_ref[u] = acc_ref[u] * shrink + jnp.dot(
                v, p.astype(jnp.bfloat16), preferred_element_type=jnp.float32
            )
            s = following

    def keys_at(k0, count):
        k = kv[pl.ds(k0, count), :HEAD_SIZE]
        return jnp.concatenate([k, k], axis=1)

    def step(t, carry):
        k0 = pl.multiple_of(anchor + t * TK, BLK)
        clear = (k0 >= low_last) & (k0 + TK - 1 <= first)

        @pl.when(clear)
        def _():
            attend(range(len(units)), keys_at(k0, TK), v_t[t], None)

        for tq in range(chip_rows // TQ):
            for piece in range(TK // TQ):
                p0 = first + tq * TQ
                from_key = pl.multiple_of(k0 + piece * TQ, BLK)
                used = (from_key <= p0 + TQ - 1) & (from_key + TQ - 1 >= start_of(p0))

                @pl.when(jnp.logical_not(clear) & used)
                def _(tq=tq, piece=piece, p0=p0, from_key=from_key):
                    kpos = from_key + lax.broadcasted_iota(jnp.int32, (TQ, TQ), 0)
                    qpos = p0 + lax.broadcasted_iota(jnp.int32, (1, TQ), 1)
                    allowed = (kpos <= qpos) & (kpos >= start_of(qpos))
                    attend(
                        [tq * GROUP + h for h in range(GROUP)],
                        keys_at(from_key, TQ),
                        v_t[t, :, piece * TQ : (piece + 1) * TQ],
                        allowed,
                    )

        return carry

    lax.fori_loop(0, (first + chip_rows - anchor + TK - 1) // TK, step, 0)
    for tq in range(chip_rows // TQ):
        side = tq * TQ // per_dev
        r0 = tq * TQ % per_dev
        parts = [
            (acc_ref[tq * GROUP + h] / l_ref[tq * GROUP + h]).astype(jnp.bfloat16).T for h in range(GROUP)
        ]

        def put(ref, c0, r0=r0, parts=parts):
            for h in range(GROUP):
                ref[r0 : r0 + TQ, c0 + h * HEAD_SIZE : c0 + (h + 1) * HEAD_SIZE] = parts[h]

        @pl.when(core == side)
        def _(put=put, side=side):
            put(own_out, side * GROUP * HEAD_SIZE)

        @pl.when(core != side)
        def _(put=put):
            put(send_out, 0)


def on_device(events, destination, segment, w_query, key_weight, value_weight):
    rows, width = events.shape
    ndev = lax.axis_size("ctx")
    me = lax.axis_index("ctx").astype(jnp.int32)
    core = me % 2
    chip_y = me // 2 % 4
    chip_x = me // 8
    half = GROUP * HEAD_SIZE
    shard = jax.ShapeDtypeStruct((rows + META, 2 * HEAD_SIZE), jnp.bfloat16)
    smem = pl.BlockSpec(memory_space=SMEM)
    vmem = pl.BlockSpec(memory_space=VMEM)
    hbm = pl.BlockSpec(memory_space=pl.ANY)

    def pairs(dx, dy, dc):
        return [
            (x * 8 + y * 2 + c, (x + dx) % 2 * 8 + (y + dy) % 4 * 2 + (c + dc) % 2)
            for x in range(2)
            for y in range(4)
            for c in range(2)
        ]

    up = lambda a: lax.ppermute(a, "ctx", pairs(0, 1, 0))
    down = lambda a: lax.ppermute(a, "ctx", pairs(0, -1, 0))
    across = lambda a: lax.ppermute(a, "ctx", pairs(1, 0, 0))
    swap = lambda a: lax.ppermute(a, "ctx", pairs(0, 0, 1))

    own, other = pl.pallas_call(
        kv_kernel,
        out_shape=(jax.ShapeDtypeStruct((2 * (rows + META), 2 * HEAD_SIZE), jnp.bfloat16), shard),
        in_specs=[smem, smem, smem, vmem, vmem, vmem],
        out_specs=(vmem, vmem),
        name="kv_projection",
    )(core[None], destination, segment, events, key_weight, value_weight)
    theirs = swap(other)
    q_send = pl.pallas_call(
        q_kernel,
        out_shape=jax.ShapeDtypeStruct((ndev, 2, BLK, half), jnp.bfloat16),
        in_specs=[smem, vmem, vmem, hbm],
        out_specs=hbm,
        scratch_shapes=[VMEM((2, rows, half), jnp.bfloat16), pltpu.SemaphoreType.DMA((rows // BLK * 2,))],
        name="query_projection",
    )(destination, events, w_query, own)
    mine = lax.dynamic_update_slice(own, theirs, (rows + META, 0))
    q_got = lax.all_to_all(q_send, "ctx", split_axis=0, concat_axis=0, tiled=True)
    shard_rows = rows + META
    y_down = up(mine)
    y_up = down(mine)
    x_far = across(mine)
    xd = up(x_far)
    y_two = down(y_up)
    xu = across(y_up)
    x_two_a = up(xd[:shard_rows])
    x_two_b = across(y_two[shard_rows:])
    units = 2 * rows // TQ * GROUP
    out_half = jax.ShapeDtypeStruct((rows, half), jnp.bfloat16)
    mine_out, give_out = pl.pallas_call(
        attention_kernel,
        out_shape=(jax.ShapeDtypeStruct((rows, width), jnp.bfloat16), out_half),
        in_specs=[smem] + [hbm] * 10,
        out_specs=(vmem, vmem),
        scratch_shapes=[
            VMEM((ndev * rows + TK, 2 * HEAD_SIZE), jnp.bfloat16),
            VMEM((ndev * rows // TK + 1, HEAD_SIZE, TK), jnp.bfloat16),
            VMEM((2 * rows, half), jnp.bfloat16),
            VMEM((units, 2 * HEAD_SIZE, TQ), jnp.bfloat16),
            VMEM((16, META, 2 * HEAD_SIZE), jnp.bfloat16),
            VMEM((16, HEAD_SIZE), jnp.int32),
            SMEM((16, HEAD_SIZE), jnp.int32),
            SMEM((ndev * rows // BLK,), jnp.int32),
            VMEM((units, 1, TQ), jnp.float32),
            VMEM((units, 1, TQ), jnp.float32),
            VMEM((units, HEAD_SIZE, TQ), jnp.float32),
            pltpu.SemaphoreType.DMA((1,)),
            pltpu.SemaphoreType.DMA((16,)),
        ],
        name="attention",
    )(
        jnp.stack([chip_x, chip_y, core]),
        mine, y_down, y_up, x_far, xd, y_two, xu, x_two_a, x_two_b, q_got,
    )
    got = swap(give_out)
    return lax.dynamic_update_slice(mine_out, got, (jnp.int32(0), (1 - core) * half))


def solution(mesh):
    return jax.shard_map(
        on_device,
        mesh=mesh,
        in_specs=(P(("dp", "ctx"), None), P(("dp", "ctx")), P(("dp", "ctx")), P(), P(), P()),
        out_specs=P(("dp", "ctx"), None),
        check_vma=False,
    )
```

```python
import math

import jax
import jax.numpy as jnp
from jax import lax
from jax.experimental import pallas as pl
from jax.experimental.pallas import tpu as pltpu
from jax.sharding import PartitionSpec as P


QUERY_HEADS = 8
KEY_VALUE_HEADS = 2
HEAD_SIZE = 128
GROUP = QUERY_HEADS // KEY_VALUE_HEADS
BLK = 64
META = 16
NEGATIVE_FILL = -1e30
SCALE2 = math.log2(math.e) / math.sqrt(HEAD_SIZE)
TK = 1024
TQ = 512


VMEM = pltpu.VMEM
SMEM = pltpu.SMEM


def lower_bound(ref, value, size):
    low = jnp.int32(0)
    step = size
    while step >= 1:
        probe = low + step
        inside = probe <= size
        entry = ref[jnp.minimum(probe, size) - 1]
        low = jnp.where(inside & (entry < value), probe, low)
        step //= 2
    return low


def kv_kernel(core_ref, dest_ref, seg_ref, ev_ref, kw_ref, vw_ref, own_ref, send_ref):
    rows = ev_ref.shape[0]
    core = core_ref[0]
    events = ev_ref[...]
    keys = jnp.dot(events, kw_ref[...], preferred_element_type=jnp.float32).astype(jnp.bfloat16)
    values = jnp.dot(events, vw_ref[...], preferred_element_type=jnp.float32).astype(jnp.bfloat16)

    def put(ref, head):
        cols = slice(head * HEAD_SIZE, (head + 1) * HEAD_SIZE)
        ref[:rows, :HEAD_SIZE] = keys[:, cols]
        ref[:rows, HEAD_SIZE:] = values[:, cols]

    @pl.when(core == 0)
    def _():
        put(own_ref, 0)
        put(send_ref, 1)

    @pl.when(core != 0)
    def _():
        put(own_ref, 1)
        put(send_ref, 0)

    lane = lax.broadcasted_iota(jnp.int32, (META, 2 * HEAD_SIZE), 1)
    meta = jnp.zeros((META, 2 * HEAD_SIZE), jnp.int32)
    for b in range(rows // BLK):
        meta = jnp.where(lane == b, dest_ref[b * BLK] // BLK, meta)
    for s in range(3):
        below = lower_bound(seg_ref, s + 1, rows)
        first = jnp.minimum(below, rows // 2)
        meta = jnp.where(lane == 16 + 2 * s, first, meta)
        meta = jnp.where(lane == 17 + 2 * s, below - first, meta)
    packed = meta.astype(jnp.float32).astype(jnp.bfloat16)
    own_ref[rows : rows + META, :] = packed
    send_ref[rows:, :] = packed


def q_kernel(dest_ref, ev_ref, wq_ref, after_ref, out_ref, q_ref, sem):
    del after_ref
    rows = ev_ref.shape[0]
    half = GROUP * HEAD_SIZE
    for g in range(KEY_VALUE_HEADS):
        q_ref[g] = jnp.dot(
            ev_ref[...], wq_ref[:, g * half : (g + 1) * half], preferred_element_type=jnp.float32
        ).astype(jnp.bfloat16)
    copies = []
    for b in range(rows // BLK):
        target = dest_ref[b * BLK] // rows
        chip = target // 2
        side = target % 2
        for g in range(KEY_VALUE_HEADS):
            copies.append(
                pltpu.make_async_copy(
                    q_ref.at[g, pl.ds(b * BLK, BLK), :],
                    out_ref.at[chip * 2 + g, side],
                    sem.at[b * KEY_VALUE_HEADS + g],
                )
            )
            copies[-1].start()
    for copy in copies:
        copy.wait()


def attention_kernel(where_ref, *refs):
    shards = refs[:8]
    last_ref, q_in_ref, own_out, send_out = refs[8:12]
    kv, v_t, q_buf, q_t, meta_bf, meta_int, table, origin, m_ref, l_ref, acc_ref, sem, meta_sem = refs[12:]
    chip_x, chip_y, core = where_ref[0], where_ref[1], where_ref[2]
    per_dev = (kv.shape[0] - TK) // 16
    shard_rows = per_dev + META
    blocks = per_dev // BLK
    offsets = [(0, 0), (0, 3), (0, 1), (1, 0), (1, 3), (0, 2), (1, 1), (1, 2)]

    def source(i, h):
        if i < 7:
            return shards[i], h * shard_rows
        return (shards[7], 0) if h == 0 else (last_ref, 0)

    fetches = []
    for i in range(8):
        for h in range(2):
            ref, base = source(i, h)
            copy = pltpu.make_async_copy(
                ref.at[pl.ds(base + per_dev, META), :], meta_bf.at[i * 2 + h], meta_sem.at[i * 2 + h]
            )
            copy.start()
            fetches.append(copy)
    for copy in fetches:
        copy.wait()
    meta = meta_bf[:, 0, :HEAD_SIZE].astype(jnp.float32).astype(jnp.int32)
    lane = lax.broadcasted_iota(jnp.int32, meta.shape, 1)
    total = jnp.sum(meta, axis=0, keepdims=True)
    meta_int[...] = jnp.where(lane < 16, meta, jnp.broadcast_to(total, meta.shape))
    copy = pltpu.make_async_copy(meta_int, table, meta_sem.at[0])
    copy.start()
    copy.wait()

    my_chip = chip_x * 4 + chip_y
    for i, (dx, dy) in enumerate(offsets):
        chip = (chip_x + dx) % 2 * 4 + (chip_y + dy) % 4
        for h in range(2):
            ref, base = source(i, h)
            device = chip * 2 + (core if h == 0 else 1 - core)

            def place(b, carry, ref=ref, base=base, device=device, i=i, h=h):
                j = table[i * 2 + h, b]
                pltpu.make_async_copy(
                    ref.at[pl.ds(base + b * BLK, BLK), :], kv.at[pl.ds(j * BLK, BLK), :], sem.at[0]
                ).start()

                origin[j] = device
                return carry

            lax.fori_loop(0, blocks, place, 0, unroll=True)
    q_copies = []
    for n in range(2 * blocks):
        copy = pltpu.make_async_copy(
            q_in_ref.at[origin[my_chip * 2 * blocks + n], n // blocks],
            q_buf.at[n * BLK : (n + 1) * BLK, :],
            meta_sem.at[n],
        )
        copy.start()
        q_copies.append(copy)
    bound = [table[0, 16 + 2 * s] + table[0, 17 + 2 * s] for s in range(3)]

    def start_of(pos):
        begin = jnp.zeros_like(pos)
        for b in bound:
            begin = jnp.where(pos >= b, jnp.maximum(begin, b), begin)
        return begin

    rows_all = pl.ds(0, 16 * per_dev)
    kv[16 * per_dev :, :] = jnp.zeros((TK, 2 * HEAD_SIZE), jnp.bfloat16)

    chip_rows = 2 * per_dev
    first = my_chip * chip_rows
    low_first = start_of(first)
    anchor = low_first // TK * TK

    for copy in q_copies:
        copy.wait()
    units = [(tq, h) for tq in range(chip_rows // TQ) for h in range(GROUP)]
    for u, (tq, h) in enumerate(units):
        q = q_buf[tq * TQ : (tq + 1) * TQ, h * HEAD_SIZE : (h + 1) * HEAD_SIZE]
        q = q.astype(jnp.float32) * SCALE2
        high = q.astype(jnp.bfloat16)
        q_t[u, :HEAD_SIZE] = high.T
        q_t[u, HEAD_SIZE:] = (q - high.astype(jnp.float32)).astype(jnp.bfloat16).T
        m_ref[u] = jnp.full((1, TQ), NEGATIVE_FILL, jnp.float32)
        l_ref[u] = jnp.zeros((1, TQ), jnp.float32)
        acc_ref[u] = jnp.zeros((HEAD_SIZE, TQ), jnp.float32)
    pltpu.make_async_copy(kv.at[rows_all], kv.at[rows_all], sem.at[0]).wait()

    def turn(t, carry):
        rows = pl.ds(pl.multiple_of(anchor + t * TK, BLK), TK)
        v_t[t] = kv[rows, HEAD_SIZE:].T
        return carry

    lax.fori_loop(0, (first + chip_rows - anchor + TK - 1) // TK, turn, 0)


    def attend(work, k, v, allowed=None, columns=None):
        def score(u):
            s = jnp.dot(k, q_t[u], preferred_element_type=jnp.float32)
            return s if allowed is None else jnp.where(allowed, s, NEGATIVE_FILL)

        s = score(work[0])
        for n, u in enumerate(work):
            following = score(work[n + 1]) if n + 1 < len(work) else None
            m_old = m_ref[u]
            m_new = jnp.maximum(m_old, jnp.max(s, axis=0, keepdims=True))
            shift = m_new
            if columns is not None:
                shift = jnp.where(columns[units[u][0]], m_new, -NEGATIVE_FILL)
                m_new = jnp.where(columns[units[u][0]], m_new, m_old)
            p = jnp.exp2(s - shift)
            shrink = jnp.exp2(m_old - m_new)
            m_ref[u] = m_new
            l_ref[u] = l_ref[u] * shrink + jnp.sum(p, axis=0, keepdims=True)
            acc_ref[u] = acc_ref[u] * shrink + jnp.dot(
                v, p.astype(jnp.bfloat16), preferred_element_type=jnp.float32
            )
            s = following

    def keys_at(k0, count):
        k = kv[pl.ds(k0, count), :HEAD_SIZE]
        return jnp.concatenate([k, k], axis=1)

    def step(t, carry):
        k0 = pl.multiple_of(anchor + t * TK, BLK)
        clear = (k0 >= low_first) & (k0 + TK <= first)

        @pl.when(clear)
        def _():
            columns = []
            for tq in range(chip_rows // TQ):
                qpos = first + tq * TQ + lax.broadcasted_iota(jnp.int32, (1, TQ), 1)
                columns.append(start_of(qpos) <= k0)
            attend(range(len(units)), keys_at(k0, TK), v_t[t], columns=columns)

        for tq in range(chip_rows // TQ):
            for piece in range(TK // TQ):
                p0 = first + tq * TQ
                from_key = pl.multiple_of(k0 + piece * TQ, BLK)
                used = (from_key <= p0 + TQ - 1) & (from_key + TQ - 1 >= start_of(p0))

                @pl.when(jnp.logical_not(clear) & used)
                def _(tq=tq, piece=piece, p0=p0, from_key=from_key):
                    kpos = from_key + lax.broadcasted_iota(jnp.int32, (TQ, TQ), 0)
                    qpos = p0 + lax.broadcasted_iota(jnp.int32, (1, TQ), 1)
                    allowed = (kpos <= qpos) & (kpos >= start_of(qpos))
                    attend(
                        [tq * GROUP + h for h in range(GROUP)],
                        keys_at(from_key, TQ),
                        v_t[t, :, piece * TQ : (piece + 1) * TQ],
                        allowed=allowed,
                    )

        return carry

    lax.fori_loop(0, (first + chip_rows - anchor + TK - 1) // TK, step, 0)
    for tq in range(chip_rows // TQ):
        side = tq * TQ // per_dev
        r0 = tq * TQ % per_dev
        parts = [
            (acc_ref[tq * GROUP + h] / l_ref[tq * GROUP + h]).astype(jnp.bfloat16).T for h in range(GROUP)
        ]

        def put(ref, c0, r0=r0, parts=parts):
            for h in range(GROUP):
                ref[r0 : r0 + TQ, c0 + h * HEAD_SIZE : c0 + (h + 1) * HEAD_SIZE] = parts[h]

        @pl.when(core == side)
        def _(put=put, side=side):
            put(own_out, side * GROUP * HEAD_SIZE)

        @pl.when(core != side)
        def _(put=put):
            put(send_out, 0)


def on_device(events, destination, segment, w_query, key_weight, value_weight):
    rows, width = events.shape
    ndev = lax.axis_size("ctx")
    me = lax.axis_index("ctx").astype(jnp.int32)
    core = me % 2
    chip_y = me // 2 % 4
    chip_x = me // 8
    half = GROUP * HEAD_SIZE
    shard = jax.ShapeDtypeStruct((rows + META, 2 * HEAD_SIZE), jnp.bfloat16)
    smem = pl.BlockSpec(memory_space=SMEM)
    vmem = pl.BlockSpec(memory_space=VMEM)
    hbm = pl.BlockSpec(memory_space=pl.ANY)

    def pairs(dx, dy, dc):
        return [
            (x * 8 + y * 2 + c, (x + dx) % 2 * 8 + (y + dy) % 4 * 2 + (c + dc) % 2)
            for x in range(2)
            for y in range(4)
            for c in range(2)
        ]

    up = lambda a: lax.ppermute(a, "ctx", pairs(0, 1, 0))
    down = lambda a: lax.ppermute(a, "ctx", pairs(0, -1, 0))
    across = lambda a: lax.ppermute(a, "ctx", pairs(1, 0, 0))
    swap = lambda a: lax.ppermute(a, "ctx", pairs(0, 0, 1))

    own, other = pl.pallas_call(
        kv_kernel,
        out_shape=(jax.ShapeDtypeStruct((2 * (rows + META), 2 * HEAD_SIZE), jnp.bfloat16), shard),
        in_specs=[smem, smem, smem, vmem, vmem, vmem],
        out_specs=(vmem, vmem),
        name="kv_projection",
    )(core[None], destination, segment, events, key_weight, value_weight)
    theirs = swap(other)
    mine = lax.dynamic_update_slice(own, theirs, (rows + META, 0))
    q_send = pl.pallas_call(
        q_kernel,
        out_shape=jax.ShapeDtypeStruct((ndev, 2, BLK, half), jnp.bfloat16),
        in_specs=[smem, vmem, vmem, hbm],
        out_specs=hbm,
        scratch_shapes=[VMEM((2, rows, half), jnp.bfloat16), pltpu.SemaphoreType.DMA((rows // BLK * 2,))],
        name="query_projection",
    )(destination, events, w_query, mine)
    q_got = lax.all_to_all(q_send, "ctx", split_axis=0, concat_axis=0, tiled=True)
    shard_rows = rows + META
    y_down = up(mine)
    y_up = down(mine)
    x_far = across(mine)
    xd = up(x_far)
    y_two = down(y_up)
    xu = across(y_up)
    x_two_a = up(xd[:shard_rows])
    x_two_b = across(y_two[shard_rows:])
    units = 2 * rows // TQ * GROUP
    out_half = jax.ShapeDtypeStruct((rows, half), jnp.bfloat16)
    mine_out, give_out = pl.pallas_call(
        attention_kernel,
        out_shape=(jax.ShapeDtypeStruct((rows, width), jnp.bfloat16), out_half),
        in_specs=[smem] + [hbm] * 10,
        out_specs=(vmem, vmem),
        scratch_shapes=[
            VMEM((ndev * rows + TK, 2 * HEAD_SIZE), jnp.bfloat16),
            VMEM((ndev * rows // TK + 1, HEAD_SIZE, TK), jnp.bfloat16),
            VMEM((2 * rows, half), jnp.bfloat16),
            VMEM((units, 2 * HEAD_SIZE, TQ), jnp.bfloat16),
            VMEM((16, META, 2 * HEAD_SIZE), jnp.bfloat16),
            VMEM((16, HEAD_SIZE), jnp.int32),
            SMEM((16, HEAD_SIZE), jnp.int32),
            SMEM((ndev * rows // BLK,), jnp.int32),
            VMEM((units, 1, TQ), jnp.float32),
            VMEM((units, 1, TQ), jnp.float32),
            VMEM((units, HEAD_SIZE, TQ), jnp.float32),
            pltpu.SemaphoreType.DMA((1,)),
            pltpu.SemaphoreType.DMA((16,)),
        ],
        name="attention",
    )(
        jnp.stack([chip_x, chip_y, core]),
        mine, y_down, y_up, x_far, xd, y_two, xu, x_two_a, x_two_b, q_got,
    )
    got = swap(give_out)
    return lax.dynamic_update_slice(mine_out, got, (jnp.int32(0), (1 - core) * half))


def solution(mesh):
    return jax.shard_map(
        on_device,
        mesh=mesh,
        in_specs=(P(("dp", "ctx"), None), P(("dp", "ctx")), P(("dp", "ctx")), P(), P(), P()),
        out_specs=P(("dp", "ctx"), None),
        check_vma=False,
    )
```

```python
import math

import jax
import jax.numpy as jnp
from jax import lax
from jax.experimental import pallas as pl
from jax.experimental.pallas import tpu as pltpu
from jax.sharding import PartitionSpec as P


QUERY_HEADS = 8
KEY_VALUE_HEADS = 2
HEAD_SIZE = 128
GROUP = QUERY_HEADS // KEY_VALUE_HEADS
BLK = 64
META = 16
NEGATIVE_FILL = -1e30
SCALE2 = math.log2(math.e) / math.sqrt(HEAD_SIZE)
TK = 1024
TQ = 512


VMEM = pltpu.VMEM
SMEM = pltpu.SMEM


def lower_bound(ref, value, size):
    low = jnp.int32(0)
    step = size
    while step >= 1:
        probe = low + step
        inside = probe <= size
        entry = ref[jnp.minimum(probe, size) - 1]
        low = jnp.where(inside & (entry < value), probe, low)
        step //= 2
    return low


def kv_kernel(core_ref, dest_ref, seg_ref, ev_ref, kw_ref, vw_ref, own_ref, send_ref):
    rows = ev_ref.shape[0]
    core = core_ref[0]
    events = ev_ref[...]
    keys = jnp.dot(events, kw_ref[...], preferred_element_type=jnp.float32).astype(jnp.bfloat16)
    values = jnp.dot(events, vw_ref[...], preferred_element_type=jnp.float32).astype(jnp.bfloat16)

    def put(ref, head):
        cols = slice(head * HEAD_SIZE, (head + 1) * HEAD_SIZE)
        ref[:rows, :HEAD_SIZE] = keys[:, cols]
        ref[:rows, HEAD_SIZE:] = values[:, cols]

    @pl.when(core == 0)
    def _():
        put(own_ref, 0)
        put(send_ref, 1)

    @pl.when(core != 0)
    def _():
        put(own_ref, 1)
        put(send_ref, 0)

    lane = lax.broadcasted_iota(jnp.int32, (META, 2 * HEAD_SIZE), 1)
    meta = jnp.zeros((META, 2 * HEAD_SIZE), jnp.int32)
    for b in range(rows // BLK):
        meta = jnp.where(lane == b, dest_ref[b * BLK] // BLK, meta)
    for s in range(3):
        below = lower_bound(seg_ref, s + 1, rows)
        first = jnp.minimum(below, rows // 2)
        meta = jnp.where(lane == 16 + 2 * s, first, meta)
        meta = jnp.where(lane == 17 + 2 * s, below - first, meta)
    packed = meta.astype(jnp.float32).astype(jnp.bfloat16)
    own_ref[rows : rows + META, :] = packed
    send_ref[rows:, :] = packed


def q_kernel(dest_ref, ev_ref, wq_ref, after_ref, out_ref, q_ref, sem):
    del after_ref
    rows = ev_ref.shape[0]
    half = GROUP * HEAD_SIZE
    for g in range(KEY_VALUE_HEADS):
        q_ref[g] = jnp.dot(
            ev_ref[...], wq_ref[:, g * half : (g + 1) * half], preferred_element_type=jnp.float32
        ).astype(jnp.bfloat16)
    copies = []
    for b in range(rows // BLK):
        target = dest_ref[b * BLK] // rows
        chip = target // 2
        side = target % 2
        for g in range(KEY_VALUE_HEADS):
            copies.append(
                pltpu.make_async_copy(
                    q_ref.at[g, pl.ds(b * BLK, BLK), :],
                    out_ref.at[chip * 2 + g, side],
                    sem.at[b * KEY_VALUE_HEADS + g],
                )
            )
            copies[-1].start()
    for copy in copies:
        copy.wait()


def attention_kernel(where_ref, *refs):
    shards = refs[:8]
    last_ref, q_in_ref, own_out, send_out = refs[8:12]
    kv, v_t, q_buf, q_t, meta_bf, meta_int, table, origin, m_ref, l_ref, acc_ref, sem, meta_sem = refs[12:]
    chip_x, chip_y, core = where_ref[0], where_ref[1], where_ref[2]
    per_dev = (kv.shape[0] - TK) // 16
    shard_rows = per_dev + META
    blocks = per_dev // BLK
    offsets = [(0, 0), (0, 3), (0, 1), (1, 0), (1, 3), (0, 2), (1, 1), (1, 2)]

    def source(i, h):
        if i < 7:
            return shards[i], h * shard_rows
        return (shards[7], 0) if h == 0 else (last_ref, 0)

    fetches = []
    for i in range(8):
        for h in range(2):
            ref, base = source(i, h)
            copy = pltpu.make_async_copy(
                ref.at[pl.ds(base + per_dev, META), :], meta_bf.at[i * 2 + h], meta_sem.at[i * 2 + h]
            )
            copy.start()
            fetches.append(copy)
    for copy in fetches:
        copy.wait()
    meta = meta_bf[:, 0, :HEAD_SIZE].astype(jnp.float32).astype(jnp.int32)
    lane = lax.broadcasted_iota(jnp.int32, meta.shape, 1)
    total = jnp.sum(meta, axis=0, keepdims=True)
    meta_int[...] = jnp.where(lane < 16, meta, jnp.broadcast_to(total, meta.shape))
    copy = pltpu.make_async_copy(meta_int, table, meta_sem.at[0])
    copy.start()
    copy.wait()

    my_chip = chip_x * 4 + chip_y
    for i, (dx, dy) in enumerate(offsets):
        chip = (chip_x + dx) % 2 * 4 + (chip_y + dy) % 4
        for h in range(2):
            ref, base = source(i, h)
            device = chip * 2 + (core if h == 0 else 1 - core)

            def place(b, carry, ref=ref, base=base, device=device, i=i, h=h):
                j = table[i * 2 + h, b]
                pltpu.make_async_copy(
                    ref.at[pl.ds(base + b * BLK, BLK), :], kv.at[pl.ds(j * BLK, BLK), :], sem.at[0]
                ).start()

                origin[j] = device
                return carry

            lax.fori_loop(0, blocks, place, 0, unroll=True)
    q_copies = []
    for n in range(2 * blocks):
        copy = pltpu.make_async_copy(
            q_in_ref.at[origin[my_chip * 2 * blocks + n], n // blocks],
            q_buf.at[n * BLK : (n + 1) * BLK, :],
            meta_sem.at[n],
        )
        copy.start()
        q_copies.append(copy)
    bound = [table[0, 16 + 2 * s] + table[0, 17 + 2 * s] for s in range(3)]

    def start_of(pos):
        begin = jnp.zeros_like(pos)
        for b in bound:
            begin = jnp.where(pos >= b, jnp.maximum(begin, b), begin)
        return begin

    rows_all = pl.ds(0, 16 * per_dev)
    kv[16 * per_dev :, :] = jnp.zeros((TK, 2 * HEAD_SIZE), jnp.bfloat16)

    chip_rows = 2 * per_dev
    first = my_chip * chip_rows
    low_first = start_of(first)
    anchor = low_first // TK * TK

    for copy in q_copies:
        copy.wait()
    units = [(tq, h) for tq in range(chip_rows // TQ) for h in range(GROUP)]
    for u, (tq, h) in enumerate(units):
        q = q_buf[tq * TQ : (tq + 1) * TQ, h * HEAD_SIZE : (h + 1) * HEAD_SIZE]
        q = q.astype(jnp.float32) * SCALE2
        high = q.astype(jnp.bfloat16)
        q_t[u, :HEAD_SIZE] = high.T
        q_t[u, HEAD_SIZE:] = (q - high.astype(jnp.float32)).astype(jnp.bfloat16).T
        m_ref[u] = jnp.full((1, TQ), NEGATIVE_FILL, jnp.float32)
        l_ref[u] = jnp.zeros((1, TQ), jnp.float32)
        acc_ref[u] = jnp.zeros((HEAD_SIZE, TQ), jnp.float32)
    pltpu.make_async_copy(kv.at[rows_all], kv.at[rows_all], sem.at[0]).wait()

    def turn(t, carry):
        rows = pl.ds(pl.multiple_of(anchor + t * TK, BLK), TK)
        v_t[t] = kv[rows, HEAD_SIZE:].T
        return carry

    lax.fori_loop(0, (first + chip_rows - anchor + TK - 1) // TK, turn, 0)


    def attend(work, k, v, allowed=None, columns=None):
        def score(u):
            s = jnp.dot(k, q_t[u], preferred_element_type=jnp.float32)
            return s if allowed is None else jnp.where(allowed[units[u][0]], s, NEGATIVE_FILL)

        s = score(work[0])
        for n, u in enumerate(work):
            following = score(work[n + 1]) if n + 1 < len(work) else None
            m_old = m_ref[u]
            m_new = jnp.maximum(m_old, jnp.max(s, axis=0, keepdims=True))
            shift = m_new
            if columns is not None:
                shift = jnp.where(columns[units[u][0]], m_new, -NEGATIVE_FILL)
                m_new = jnp.where(columns[units[u][0]], m_new, m_old)
            p = jnp.exp2(s - shift)
            shrink = jnp.exp2(m_old - m_new)
            m_ref[u] = m_new
            l_ref[u] = l_ref[u] * shrink + jnp.sum(p, axis=0, keepdims=True)
            acc_ref[u] = acc_ref[u] * shrink + jnp.dot(
                v, p.astype(jnp.bfloat16), preferred_element_type=jnp.float32
            )
            s = following

    def keys_at(k0, count):
        k = kv[pl.ds(k0, count), :HEAD_SIZE]
        return jnp.concatenate([k, k], axis=1)

    def step(t, carry):
        k0 = pl.multiple_of(anchor + t * TK, BLK)
        clear = (k0 >= low_first) & (k0 + TK <= first)

        @pl.when(clear)
        def _():
            columns = []
            for tq in range(chip_rows // TQ):
                qpos = first + tq * TQ + lax.broadcasted_iota(jnp.int32, (1, TQ), 1)
                columns.append(start_of(qpos) <= k0)
            attend(range(len(units)), keys_at(k0, TK), v_t[t], columns=columns)

        for piece in range(TK // TQ):
            from_key = pl.multiple_of(k0 + piece * TQ, BLK)

            def masked(tiles, piece=piece, from_key=from_key):
                kpos = from_key + lax.broadcasted_iota(jnp.int32, (TQ, TQ), 0)
                allowed = {}
                for tq in tiles:
                    qpos = first + tq * TQ + lax.broadcasted_iota(jnp.int32, (1, TQ), 1)
                    allowed[tq] = (kpos <= qpos) & (kpos >= start_of(qpos))
                attend(
                    [u for u, (tq, _) in enumerate(units) if tq in tiles],
                    keys_at(from_key, TQ),
                    v_t[t, :, piece * TQ : (piece + 1) * TQ],
                    allowed=allowed,
                )

            def used(tq, from_key=from_key):
                p0 = first + tq * TQ
                return (from_key <= p0 + TQ - 1) & (from_key + TQ - 1 >= start_of(p0))

            @pl.when(jnp.logical_not(clear) & used(0))
            def _(masked=masked):
                masked((0, 1))

            @pl.when(jnp.logical_not(clear) & jnp.logical_not(used(0)) & used(1))
            def _(masked=masked):
                masked((1,))

        return carry

    lax.fori_loop(0, (first + chip_rows - anchor + TK - 1) // TK, step, 0)
    for tq in range(chip_rows // TQ):
        side = tq * TQ // per_dev
        r0 = tq * TQ % per_dev
        parts = [
            (acc_ref[tq * GROUP + h] / l_ref[tq * GROUP + h]).astype(jnp.bfloat16).T for h in range(GROUP)
        ]

        def put(ref, c0, r0=r0, parts=parts):
            for h in range(GROUP):
                ref[r0 : r0 + TQ, c0 + h * HEAD_SIZE : c0 + (h + 1) * HEAD_SIZE] = parts[h]

        @pl.when(core == side)
        def _(put=put, side=side):
            put(own_out, side * GROUP * HEAD_SIZE)

        @pl.when(core != side)
        def _(put=put):
            put(send_out, 0)


def on_device(events, destination, segment, w_query, key_weight, value_weight):
    rows, width = events.shape
    ndev = lax.axis_size("ctx")
    me = lax.axis_index("ctx").astype(jnp.int32)
    core = me % 2
    chip_y = me // 2 % 4
    chip_x = me // 8
    half = GROUP * HEAD_SIZE
    shard = jax.ShapeDtypeStruct((rows + META, 2 * HEAD_SIZE), jnp.bfloat16)
    smem = pl.BlockSpec(memory_space=SMEM)
    vmem = pl.BlockSpec(memory_space=VMEM)
    hbm = pl.BlockSpec(memory_space=pl.ANY)

    def pairs(dx, dy, dc):
        return [
            (x * 8 + y * 2 + c, (x + dx) % 2 * 8 + (y + dy) % 4 * 2 + (c + dc) % 2)
            for x in range(2)
            for y in range(4)
            for c in range(2)
        ]

    up = lambda a: lax.ppermute(a, "ctx", pairs(0, 1, 0))
    down = lambda a: lax.ppermute(a, "ctx", pairs(0, -1, 0))
    across = lambda a: lax.ppermute(a, "ctx", pairs(1, 0, 0))
    swap = lambda a: lax.ppermute(a, "ctx", pairs(0, 0, 1))

    own, other = pl.pallas_call(
        kv_kernel,
        out_shape=(jax.ShapeDtypeStruct((2 * (rows + META), 2 * HEAD_SIZE), jnp.bfloat16), shard),
        in_specs=[smem, smem, smem, vmem, vmem, vmem],
        out_specs=(vmem, vmem),
        name="kv_projection",
    )(core[None], destination, segment, events, key_weight, value_weight)
    theirs = swap(other)
    mine = lax.dynamic_update_slice(own, theirs, (rows + META, 0))
    q_send = pl.pallas_call(
        q_kernel,
        out_shape=jax.ShapeDtypeStruct((ndev, 2, BLK, half), jnp.bfloat16),
        in_specs=[smem, vmem, vmem, hbm],
        out_specs=hbm,
        scratch_shapes=[VMEM((2, rows, half), jnp.bfloat16), pltpu.SemaphoreType.DMA((rows // BLK * 2,))],
        name="query_projection",
    )(destination, events, w_query, mine)
    q_got = lax.all_to_all(q_send, "ctx", split_axis=0, concat_axis=0, tiled=True)
    shard_rows = rows + META
    y_down = up(mine)
    y_up = down(mine)
    x_far = across(mine)
    xd = up(x_far)
    y_two = down(y_up)
    xu = across(y_up)
    x_two_a = up(xd[:shard_rows])
    x_two_b = across(y_two[shard_rows:])
    units = 2 * rows // TQ * GROUP
    out_half = jax.ShapeDtypeStruct((rows, half), jnp.bfloat16)
    mine_out, give_out = pl.pallas_call(
        attention_kernel,
        out_shape=(jax.ShapeDtypeStruct((rows, width), jnp.bfloat16), out_half),
        in_specs=[smem] + [hbm] * 10,
        out_specs=(vmem, vmem),
        scratch_shapes=[
            VMEM((ndev * rows + TK, 2 * HEAD_SIZE), jnp.bfloat16),
            VMEM((ndev * rows // TK + 1, HEAD_SIZE, TK), jnp.bfloat16),
            VMEM((2 * rows, half), jnp.bfloat16),
            VMEM((units, 2 * HEAD_SIZE, TQ), jnp.bfloat16),
            VMEM((16, META, 2 * HEAD_SIZE), jnp.bfloat16),
            VMEM((16, HEAD_SIZE), jnp.int32),
            SMEM((16, HEAD_SIZE), jnp.int32),
            SMEM((ndev * rows // BLK,), jnp.int32),
            VMEM((units, 1, TQ), jnp.float32),
            VMEM((units, 1, TQ), jnp.float32),
            VMEM((units, HEAD_SIZE, TQ), jnp.float32),
            pltpu.SemaphoreType.DMA((1,)),
            pltpu.SemaphoreType.DMA((16,)),
        ],
        name="attention",
    )(
        jnp.stack([chip_x, chip_y, core]),
        mine, y_down, y_up, x_far, xd, y_two, xu, x_two_a, x_two_b, q_got,
    )
    got = swap(give_out)
    return lax.dynamic_update_slice(mine_out, got, (jnp.int32(0), (1 - core) * half))


def solution(mesh):
    return jax.shard_map(
        on_device,
        mesh=mesh,
        in_specs=(P(("dp", "ctx"), None), P(("dp", "ctx")), P(("dp", "ctx")), P(), P(), P()),
        out_specs=P(("dp", "ctx"), None),
        check_vma=False,
    )
```
